256 devices in a mesh: curve: 128 (over y_lo, z, x, core), dp: 2 (over y_hi).
Axes of the slice: x: 4, y: 4 (y_hi: 2, y_lo: 2; y = y_hi * 2 + y_lo), z: 8, core: 2. Of those that a mesh axis runs over, the one named last changes fastest.
Arguments:
- points: bfloat16 [2, 65536, 512], P('dp', 'curve'), may hold values from -24 to 24
- grad_out: bfloat16 [2, 65536, 512], P('dp', 'curve'), may hold values from -6 to 6
- dest_dev: int32 [2, 65536], P('dp', 'curve'), may hold values from 0 to 127, as said below
- dest_row: int32 [2, 65536], P('dp', 'curve'), may hold values from 0 to 511
- w_qkv: bfloat16 [512, 1536], replicated, may hold values from -1 to 1
- w_out: bfloat16 [512, 512], replicated, may hold values from -0.25 to 0.25
Outputs:
- grad_points: bfloat16 [2, 65536, 512], P('dp', 'curve')
- grad_w_qkv: float32 [512, 1536], replicated
- grad_w_out: float32 [512, 512], replicated
The draws below stay inside these ranges and needn't reach their ends.
Inputs may be any that keep to these rules, and one draw needn't show every extreme that they name: `dest_dev`: together with dest_row it maps each group's scan points one to one onto the 65536 curve positions: every curve device of a group receives exactly 512 points, at most 8 of them from one scan device, and in every draw some scan device sends exactly 8 points to some curve device.
All inputs are finite; a program needn't handle non-finite values.
Results may differ from the reference program's by a relative error of at most 0.011.
The reference program's roundings to bfloat16 on the way count: a program that leaves them out, or rounds other values in their place, can miss the bound.
Values may be sent and summed in bfloat16 or wider, within the bound.
A program may use at most 64 MiB of HBM per device.

```python
import math
import jax
import jax.numpy as jnp
from jax import lax

D = 512
HEADS = 8
PATCH = 512
SHIFT = 256
TOK_DEV = 512
POINTS = 65536
N_CURVE = 128
N_DP = 2


def route_tables(key):
    n_dev = N_CURVE
    per_dev = TOK_DEV
    mean_count = per_dev // n_dev

    def one_group(group_key):
        keys_list = jax.random.split(group_key, 5)
        spread = jax.random.randint(keys_list[0], (n_dev // 2,), 0, mean_count + 1)
        spread = spread.at[0].set(mean_count)
        pattern = jnp.stack([spread, -spread], axis=1).reshape(n_dev)
        counts = mean_count + jax.random.permutation(keys_list[1], pattern)
        upper = jnp.cumsum(counts).astype(jnp.int32)
        label = jax.random.permutation(keys_list[2], n_dev).astype(jnp.int32)
        unlabel = jnp.zeros((n_dev,), jnp.int32).at[label].set(jnp.arange(n_dev, dtype=jnp.int32))
        order_src = jax.vmap(lambda single: jax.random.permutation(single, per_dev))(jax.random.split(keys_list[3], n_dev)).astype(jnp.int32)
        order_dst = jax.vmap(lambda single: jax.random.permutation(single, per_dev))(jax.random.split(keys_list[4], n_dev)).astype(jnp.int32)
        offset = jnp.searchsorted(upper, order_src, side='right').astype(jnp.int32)
        sources = jnp.arange(n_dev, dtype=jnp.int32)[:, None]
        dest_label = (label[sources] + offset) % n_dev
        dest = unlabel[dest_label]
        rows_at = order_dst[dest, order_src]
        return (dest.reshape(-1), rows_at.reshape(-1))
    group_keys = jax.random.split(jax.random.fold_in(key, 4242), N_DP)
    return jax.vmap(one_group)(group_keys)


def draw_dest_dev(key, part):
    return route_tables(key)[0]


def draw_dest_row(key, part):
    return route_tables(key)[1]


def draw_points(key, part):
    first_key = jax.random.fold_in(jax.random.fold_in(key, 17), 0)
    shape = (N_DP, POINTS, D)
    return jnp.clip(jax.random.normal(first_key, shape, jnp.float32), -4.0, 4.0).astype(jnp.bfloat16)


def draw_w_qkv(key, part):
    first_key = jax.random.fold_in(jax.random.fold_in(key, 91), 0)
    sigma = D ** (-0.5)
    return (jnp.clip(jax.random.normal(first_key, (D, 3 * D), jnp.float32), -4.0, 4.0) * sigma).astype(jnp.bfloat16)


def levels(stream_key, dims, cuts, low, high):
    gain = 1.0
    for dim, parts in cuts:
        heights = jax.random.uniform(jax.random.fold_in(jax.random.fold_in(stream_key, 6), dim), (parts,), jnp.float32, low / len(cuts), high / len(cuts))
        gain = gain * jnp.repeat(jnp.exp(heights), dims[dim] // parts).reshape((-1,) + (1,) * (len(dims) - 1 - dim))
    return gain


def scatter_about(stream_key, shape, scale, reach, cuts=(), held_as=jnp.bfloat16):
    values = scale * jax.random.normal(stream_key, shape, jnp.float32)
    if cuts:
        values = values * levels(stream_key, shape, cuts, -0.22, 0.18)
    return jnp.clip(values, -reach, reach).astype(held_as)


def setup_inputs(seed: int = 0) -> dict:
    key_of = jax.random.split(jax.random.key(seed), 7)
    points = draw_points(jax.random.fold_in(key_of[6], 71), 0)
    grad_out = scatter_about(key_of[1], (N_DP, POINTS, D), 1.0, 6.0, ((0, 2), (1, 128)))
    dest_dev = draw_dest_dev(jax.random.fold_in(key_of[6], 71), 0)
    dest_row = draw_dest_row(jax.random.fold_in(key_of[6], 71), 0)
    w_qkv = draw_w_qkv(jax.random.fold_in(key_of[6], 71), 0)
    w_out = scatter_about(key_of[5], (D, D), D ** -0.5, 0.25)
    return {"points": points, "grad_out": grad_out, "dest_dev": dest_dev, "dest_row": dest_row, "w_qkv": w_qkv, "w_out": w_out}


def lowered(values):
    return lax.optimization_barrier(values.astype(jnp.bfloat16)).astype(jnp.float32)

def patch_backward(qkv_patch, grad_patch):
    head_dim = D // HEADS
    scale = 1.0 / math.sqrt(head_dim)
    queries = qkv_patch[:, :D].astype(jnp.float32).reshape(PATCH, HEADS, head_dim)
    keys_all = qkv_patch[:, D:2 * D].astype(jnp.float32).reshape(PATCH, HEADS, head_dim)
    values_all = qkv_patch[:, 2 * D:].astype(jnp.float32).reshape(PATCH, HEADS, head_dim)
    grads = grad_patch.astype(jnp.float32).reshape(PATCH, HEADS, head_dim)
    scores = jnp.einsum('qhd,khd->hqk', queries, keys_all) * scale
    probs = jax.nn.softmax(scores, axis=-1)
    probs_low = lowered(probs)
    attn = jnp.einsum('hqk,khd->qhd', probs_low, values_all).astype(jnp.bfloat16)
    delta = lax.optimization_barrier(jnp.sum(grads * attn.astype(jnp.float32), axis=-1))
    grad_values = jnp.einsum('hqk,qhd->khd', probs_low, grads)
    grad_probs = jnp.einsum('qhd,khd->hqk', grads, values_all)
    grad_scores = lowered(probs * (grad_probs - jnp.transpose(delta)[:, :, None]))
    grad_queries = jnp.einsum('hqk,khd->qhd', grad_scores, keys_all) * scale
    grad_keys = jnp.einsum('hqk,qhd->khd', grad_scores, queries) * scale
    grad_qkv = jnp.concatenate([grad_queries.reshape(PATCH, D), grad_keys.reshape(PATCH, D), grad_values.reshape(PATCH, D)], axis=1)
    return (attn.reshape(PATCH, D), grad_qkv.astype(jnp.bfloat16))

def reference(points, grad_out, dest_dev, dest_row, w_qkv, w_out):
    outputs = []
    weight_qkv = jnp.zeros((D, 3 * D), jnp.float32)
    weight_out = jnp.zeros((D, D), jnp.float32)
    for group in range(N_DP):
        position = (dest_dev[group].astype(jnp.int32) * TOK_DEV + dest_row[group].astype(jnp.int32)).astype(jnp.int32)
        curve_points = jnp.zeros((POINTS, D), jnp.bfloat16).at[position].set(points[group])
        curve_grads = jnp.zeros((POINTS, D), jnp.bfloat16).at[position].set(grad_out[group])
        rolled_points = jnp.roll(curve_points, -SHIFT, axis=0)
        rolled_grads = jnp.roll(curve_grads, -SHIFT, axis=0)
        qkv = jnp.dot(rolled_points, w_qkv, preferred_element_type=jnp.float32).astype(jnp.bfloat16)
        grad_attn = jnp.dot(rolled_grads, w_out.T, preferred_element_type=jnp.float32).astype(jnp.bfloat16)
        attn, grad_qkv = lax.map(lambda pair: patch_backward(pair[0], pair[1]), (qkv.reshape(POINTS // PATCH, PATCH, 3 * D), grad_attn.reshape(POINTS // PATCH, PATCH, D)))
        attn = attn.reshape(POINTS, D)
        grad_qkv = grad_qkv.reshape(POINTS, 3 * D)
        weight_qkv = weight_qkv + jnp.dot(rolled_points.T, grad_qkv, preferred_element_type=jnp.float32)
        weight_out = weight_out + jnp.dot(attn.T, rolled_grads, preferred_element_type=jnp.float32)
        input_grads = jnp.dot(grad_qkv, w_qkv.T, preferred_element_type=jnp.float32).astype(jnp.bfloat16)
        curve_input = jnp.roll(input_grads, SHIFT, axis=0)
        outputs.append(curve_input[position])
    return (jnp.stack(outputs), weight_qkv, weight_out)
```

```python
import functools
import math

import jax
import jax.numpy as jnp
from jax import lax
from jax.experimental import pallas as pl
from jax.experimental.pallas import tpu as pltpu
from jax.sharding import PartitionSpec as P

HEADS = 8
PATCH = 512
CAP = 8
MESH = pl.DeviceIdType.MESH
BF16 = jnp.bfloat16
F32 = jnp.float32
I32 = jnp.int32
VMEM_SPEC = pl.BlockSpec(memory_space=pltpu.VMEM)
ANY_SPEC = pl.BlockSpec(memory_space=pl.ANY)


def dot_nn(a, b):
    return lax.dot_general(a, b, (((1,), (0,)), ((), ())), preferred_element_type=F32)


def dot_nt(a, b):
    return lax.dot_general(a, b, (((1,), (1,)), ((), ())), preferred_element_type=F32)


def iota(shape, dim):
    return lax.broadcasted_iota(I32, shape, dim)


def onehot(mask):
    return jnp.where(mask, 1.0, 0.0).astype(BF16)


def pack_kernel(dev_ref, row_ref, points_ref, grads_ref, send_ref, meta_ref, slot_ref):
    n_dev = send_ref.shape[0]
    rows = points_ref.shape[0]
    dev = dev_ref[...]
    mask = iota((n_dev, rows), 0) == dev
    hot = onehot(mask)
    upper = onehot(iota((rows, rows), 0) <= iota((rows, rows), 1))
    running = dot_nn(hot, upper)
    rank = jnp.sum(jnp.where(mask, running, 0.0), axis=0, keepdims=True).astype(I32) - 1
    slot_ref[...] = dev * CAP + rank
    coded = row_ref[...] + 1
    at_rank = iota((128, rows), 0) == rank
    high = jnp.where(at_rank, (coded >> 8).astype(F32), 0.0).astype(BF16)
    low = jnp.where(at_rank, (coded & 255).astype(F32), 0.0).astype(BF16)
    meta_ref[...] = dot_nt(hot, high) * 256.0 + dot_nt(hot, low)
    slot = dev * (2 * CAP) + rank
    points = points_ref[...]
    grads = grads_ref[...]
    chunk = 16

    def body(step, carry):
        base = step * (chunk * 2 * CAP)
        ids = iota((chunk * 2 * CAP, rows), 0) + base
        block = dot_nn(onehot(ids == slot), points) + dot_nn(onehot(ids == slot + CAP), grads)
        send_ref[pl.ds(step * chunk, chunk)] = block.astype(BF16).reshape(chunk, 2 * CAP, -1)
        return carry

    lax.fori_loop(0, n_dev // chunk, body, 0)


def pack(dev, row, points, grads, n_dev):
    rows, width = points.shape
    return pl.pallas_call(
        pack_kernel,
        out_shape=(
            jax.ShapeDtypeStruct((n_dev, 2 * CAP, width), BF16),
            jax.ShapeDtypeStruct((n_dev, 128), F32),
            jax.ShapeDtypeStruct((1, rows), I32),
        ),
        in_specs=[VMEM_SPEC] * 4,
        out_specs=(VMEM_SPEC,) * 3,
        name="pack",
    )(dev, row, points, grads)


def exchange_kernel(count, *refs):
    sends, gets = refs[:count], refs[count : 2 * count]
    send_sem, recv_sem, local_sem = refs[2 * count :]
    n_dev = sends[0].shape[0]
    me = lax.axis_index("curve")
    barrier = pltpu.get_barrier_semaphore()

    def greet(k, carry):
        peer = lax.rem(me + k, n_dev)
        pl.semaphore_signal(barrier, inc=1, device_id={"curve": peer}, device_id_type=MESH)
        return carry

    lax.fori_loop(1, n_dev, greet, 0)
    pl.semaphore_wait(barrier, n_dev - 1)

    def start(k, carry):
        peer = lax.rem(me + k, n_dev)
        for i in range(count):
            pltpu.make_async_remote_copy(
                src_ref=sends[i].at[peer],
                dst_ref=gets[i].at[me],
                send_sem=send_sem.at[i],
                recv_sem=recv_sem.at[i],
                device_id={"curve": peer},
                device_id_type=MESH,
            ).start()
        return carry

    lax.fori_loop(1, n_dev, start, 0)
    own = [
        pltpu.make_async_copy(sends[i].at[me], gets[i].at[me], local_sem.at[i])
        for i in range(count)
    ]
    for copy in own:
        copy.start()
    for copy in own:
        copy.wait()
    for i in range(count):
        others = pl.ds(0, n_dev - 1)
        pltpu.make_async_copy(sends[i].at[others], sends[i].at[others], send_sem.at[i]).wait()
        pltpu.make_async_copy(gets[i].at[others], gets[i].at[others], recv_sem.at[i]).wait()


def exchange(blocks, collective_id, name):
    count = len(blocks)
    return pl.pallas_call(
        functools.partial(exchange_kernel, count),
        out_shape=tuple(jax.ShapeDtypeStruct(b.shape, b.dtype) for b in blocks),
        in_specs=[VMEM_SPEC] * count,
        out_specs=(VMEM_SPEC,) * count,
        scratch_shapes=[
            pltpu.SemaphoreType.DMA((count,)),
            pltpu.SemaphoreType.DMA((count,)),
            pltpu.SemaphoreType.DMA((count,)),
        ],
        compiler_params=pltpu.CompilerParams(collective_id=collective_id, has_side_effects=True),
        name=name,
    )(*blocks)


def place_kernel(got_ref, meta_ref, low_ref, high_ref):
    n_dev, span, width = got_ref.shape
    total = n_dev * span
    half = low_ref.shape[0]
    coded = jnp.transpose(meta_ref[...])[:CAP].astype(I32)
    spread = onehot((iota((n_dev, total), 1) >> 4) == iota((n_dev, total), 0))
    high8 = (coded >> 8).astype(F32).astype(BF16)
    low8 = (coded & 255).astype(F32).astype(BF16)
    spreaded = dot_nn(high8, spread) * 256.0 + dot_nn(low8, spread)
    lane = iota((CAP, total), 1)
    row = jnp.sum(
        jnp.where((lane & (CAP - 1)) == iota((CAP, total), 0), spreaded, 0.0), axis=0, keepdims=True
    ).astype(I32) - 1
    is_grad = (iota((1, total), 1) & CAP) != 0
    row_p = jnp.where(is_grad, -1, row)
    row_g = jnp.where(is_grad, row, -1)
    got = got_ref[...].reshape(total, width)
    for index, out in enumerate((low_ref, high_ref)):
        ids = iota((half, total), 0) + index * half
        out[:, :width] = dot_nn(onehot(ids == row_p), got).astype(BF16)
        out[:, width:] = dot_nn(onehot(ids == row_g), got).astype(BF16)


def place(got, meta, half):
    width = got.shape[-1]
    shape = jax.ShapeDtypeStruct((half, 2 * width), BF16)
    return pl.pallas_call(
        place_kernel,
        out_shape=(shape, shape),
        in_specs=[VMEM_SPEC] * 2,
        out_specs=(VMEM_SPEC,) * 2,
        name="place",
    )(got, meta)


def patch_kernel(
    own_ref, next_ref, wqkv_ref, wout_ref, part_ref, igrad_own_ref, igrad_next_ref,
    x_s, g_s, q_s, k_s, v_s, ga_s, kt_s, vt_s, gat_s, attnt_s, gqkv_s,
):
    half, width2 = own_ref.shape
    width = width2 // 2
    rows = 2 * half
    x_s[:half] = own_ref[:, :width]
    x_s[half:] = next_ref[:, :width]
    g_s[:half] = own_ref[:, width:]
    g_s[half:] = next_ref[:, width:]
    pairs = width // 128
    scale = 1.0 / math.sqrt(width // HEADS)

    x = x_s[...]
    qkv = dot_nn(x, wqkv_ref[...])
    ga = dot_nt(g_s[...], wout_ref[...])
    for p in range(pairs):
        cols = slice(p * 128, (p + 1) * 128)
        q_s[p] = (qkv[:, cols].astype(BF16).astype(F32) * scale).astype(BF16)
        k = qkv[:, width + p * 128 : width + (p + 1) * 128].astype(BF16)
        v = qkv[:, 2 * width + p * 128 : 2 * width + (p + 1) * 128].astype(BF16)
        g = ga[:, cols].astype(BF16)
        k_s[p] = k
        v_s[p] = v
        ga_s[p] = g
        kt_s[p] = jnp.transpose(k)
        vt_s[p] = jnp.transpose(v)
        gat_s[p] = jnp.transpose(g)

    def body(p, carry):
        q = q_s[p]
        k = k_s[p]
        v = v_s[p]
        g = ga_s[p]
        grad_k = jnp.zeros((rows, 128), F32)
        grad_v = jnp.zeros((rows, 128), F32)
        lane = iota((rows, 128), 1) // 64
        grad_qt = []
        for h in range(2):
            part = slice(h * 64, (h + 1) * 64)
            keep = lane == h
            qh = jnp.where(keep, q.astype(F32), 0.0).astype(BF16)
            gh = jnp.where(keep, g.astype(F32), 0.0).astype(BF16)
            st = dot_nt(k, qh)
            top = jnp.max(st, axis=0, keepdims=True)
            e = jnp.exp(st - top)
            total = jnp.sum(e, axis=0, keepdims=True)
            pt = e * (1.0 / total)
            low = pt.astype(BF16)
            attnt = dot_nn(vt_s[p, part, :], low).astype(BF16)
            attnt_s[p, part, :] = attnt
            delta = jnp.sum(
                attnt.astype(F32) * gat_s[p, part, :].astype(F32), axis=0, keepdims=True
            )
            grad_v += dot_nn(low, gh)
            gpt = dot_nt(v, gh)
            gst = (pt * (gpt - delta)).astype(BF16)
            grad_k += dot_nn(gst, qh)
            grad_qt.append(dot_nn(kt_s[p, part, :], gst))
        gq = jnp.transpose(jnp.concatenate(grad_qt, axis=0) * scale)
        gqkv_s[p] = gq.astype(BF16)
        gqkv_s[pairs + p] = grad_k.astype(BF16)
        gqkv_s[2 * pairs + p] = grad_v.astype(BF16)
        return carry

    lax.fori_loop(0, pairs, body, 0)
    xt = jnp.transpose(x_s[...])
    igrad = jnp.zeros((rows, width), F32)
    for block in range(3 * pairs // 2):
        gq = jnp.concatenate([gqkv_s[2 * block], gqkv_s[2 * block + 1]], axis=1)
        part_ref[block] = dot_nn(xt, gq).astype(BF16)
        igrad += dot_nt(gq, wqkv_ref[:, block * 256 : (block + 1) * 256])
    igrad = igrad.astype(BF16)
    igrad_own_ref[...] = igrad[:half]
    igrad_next_ref[...] = igrad[half:]
    attnt = attnt_s[...].reshape(width, rows)
    pout = dot_nn(attnt, g_s[...])
    for block in range(width // 256):
        part_ref[3 * pairs // 2 + block] = pout[:, block * 256 : (block + 1) * 256].astype(BF16)


def patch_backward(own, following, w_qkv, w_out):
    half, width2 = own.shape
    width = width2 // 2
    rows = 2 * half
    pairs = width // 128
    tall = pltpu.VMEM((pairs, rows, 128), BF16)
    wide = pltpu.VMEM((pairs, 128, rows), BF16)
    return pl.pallas_call(
        patch_kernel,
        out_shape=(
            jax.ShapeDtypeStruct((4 * width // 256, width, 256), BF16),
            jax.ShapeDtypeStruct((half, width), BF16),
            jax.ShapeDtypeStruct((half, width), BF16),
        ),
        in_specs=[VMEM_SPEC] * 4,
        out_specs=(VMEM_SPEC,) * 3,
        scratch_shapes=[
            pltpu.VMEM((rows, width), BF16),
            pltpu.VMEM((rows, width), BF16),
            tall, tall, tall, tall, wide, wide, wide, wide,
            pltpu.VMEM((3 * pairs, rows, 128), BF16),
        ],
        name="patch",
    )(own, following, w_qkv, w_out)


def pick_kernel(low_ref, high_ref, meta_ref, send_ref):
    n_dev, span, width = send_ref.shape
    half = low_ref.shape[0]
    total = n_dev * span
    coded = meta_ref[...].astype(I32)
    spread = onehot((iota((total, n_dev), 0) >> 3) == iota((total, n_dev), 1))
    high = (coded >> 8).astype(F32).astype(BF16)
    low = (coded & 255).astype(F32).astype(BF16)
    spreaded = dot_nn(spread, high) * 256.0 + dot_nn(spread, low)
    own = iota((total, 128), 1) == (iota((total, 128), 0) & (CAP - 1))
    row = jnp.sum(jnp.where(own, spreaded, 0.0), axis=1, keepdims=True).astype(I32) - 1
    lane = iota((total, half), 1)
    block = dot_nn(onehot(lane == row), low_ref[...]) + dot_nn(
        onehot(lane + half == row), high_ref[...]
    )
    send_ref[...] = block.reshape(n_dev, span, width).astype(BF16)


def pick(low, high, meta):
    n_dev = meta.shape[0]
    return pl.pallas_call(
        pick_kernel,
        out_shape=jax.ShapeDtypeStruct((n_dev, CAP, low.shape[1]), BF16),
        in_specs=[VMEM_SPEC] * 3,
        out_specs=VMEM_SPEC,
        name="pick",
    )(low, high, meta)


def collect_kernel(got_ref, slot_ref, out_ref):
    n_dev, span, width = got_ref.shape
    rows = out_ref.shape[0]
    total = n_dev * span
    slot = jnp.transpose(jnp.broadcast_to(slot_ref[...].astype(F32), (128, rows)))[:, :1]
    hot = onehot(iota((rows, total), 1) == slot.astype(I32))
    got = got_ref[...].astype(F32).reshape(total, width).astype(BF16)
    out_ref[...] = dot_nn(hot, got).astype(BF16)


def collect(got, slot):
    rows = slot.shape[1]
    return pl.pallas_call(
        collect_kernel,
        out_shape=jax.ShapeDtypeStruct((rows, got.shape[2]), BF16),
        in_specs=[VMEM_SPEC] * 2,
        out_specs=VMEM_SPEC,
        name="collect",
    )(got, slot)


def reduce_kernel(
    part_ref, out_ref, r0, b0, r1, b1, r2, a3, a4, send_sem, recv_sem
):
    c = lax.axis_index("curve")
    d = lax.axis_index("dp")
    core = lax.rem(c, 2)
    x = lax.rem(c // 2, 4)
    z = lax.rem(c // 8, 8)
    y = d * 2 + c // 64
    plane = y * 4 + x
    barrier = pltpu.get_barrier_semaphore()

    def place_of(plane_id, z_id, core_id):
        yy = plane_id // 4
        xx = lax.rem(plane_id, 4)
        curve = ((lax.rem(yy, 2) * 8 + z_id) * 4 + xx) * 2 + core_id
        return {"curve": curve, "dp": yy // 2}

    def plane_peer(k):
        return lax.rem(plane + k, 16)

    def z_peer(k):
        return lax.rem(z + k, 8)

    partner = place_of(plane, z, 1 - core)

    def signal(device):
        pl.semaphore_signal(barrier, inc=1, device_id=device, device_id_type=MESH)

    signal(partner)

    def greet_plane(k, carry):
        signal(place_of(plane_peer(k), z, core))
        return carry

    def greet_z(k, carry):
        signal(place_of(plane, z_peer(k), core))
        return carry

    lax.fori_loop(1, 16, greet_plane, 0)
    lax.fori_loop(1, 8, greet_z, 0)
    pl.semaphore_wait(barrier, 23)

    def copy_to(src, dst, stage, device):
        return pltpu.make_async_remote_copy(
            src_ref=src, dst_ref=dst, send_sem=send_sem.at[stage], recv_sem=recv_sem.at[stage],
            device_id=device, device_id_type=MESH,
        )

    def wait_all(ref, count, stage):
        part = ref.at[pl.ds(0, count)]
        pltpu.make_async_copy(part, part, send_sem.at[stage]).wait()
        pltpu.make_async_copy(part, part, recv_sem.at[stage]).wait()

    first = copy_to(part_ref.at[1 - core], r0, 0, partner)
    first.start()
    first.wait()

    def add_first(i, carry):
        b0[i] = (part_ref[core, i].astype(F32) + r0[i].astype(F32)).astype(BF16)
        return carry

    lax.fori_loop(0, 16, add_first, 0)

    def send_plane(k, carry):
        peer = plane_peer(k)
        copy_to(b0.at[peer], r1.at[plane], 1, place_of(peer, z, core)).start()
        return carry

    lax.fori_loop(1, 16, send_plane, 0)
    r1[plane] = b0[plane]
    wait_all(r1, 15, 1)

    def add_plane(i, total):
        return total + r1[i].astype(F32)

    total = lax.fori_loop(0, 16, add_plane, jnp.zeros((128, 256), F32))
    b1[...] = total.astype(BF16).reshape(8, 16, 256)

    def send_z(k, carry):
        peer = z_peer(k)
        copy_to(b1.at[peer], r2.at[z], 2, place_of(plane, peer, core)).start()
        return carry

    lax.fori_loop(1, 8, send_z, 0)
    r2[z] = b1[z]
    wait_all(r2, 7, 2)
    final = jnp.sum(r2[...].astype(F32), axis=0)
    a3[z] = final.astype(BF16)

    def back_z(k, carry):
        copy_to(a3.at[z], a3.at[z], 3, place_of(plane, z_peer(k), core)).start()
        return carry

    lax.fori_loop(1, 8, back_z, 0)
    wait_all(a3, 7, 3)
    a4[plane] = a3[...].reshape(128, 256)

    def back_plane(k, carry):
        copy_to(a4.at[plane], a4.at[plane], 4, place_of(plane_peer(k), z, core)).start()
        return carry

    lax.fori_loop(1, 16, back_plane, 0)
    wait_all(a4, 15, 4)
    last = copy_to(a4, out_ref.at[core], 5, partner)
    last.start()
    out_ref[core] = a4[...]
    last.wait()


def reduce_parts(part):
    block = pltpu.VMEM((16, 128, 256), BF16)
    small = pltpu.VMEM((8, 16, 256), BF16)
    return pl.pallas_call(
        reduce_kernel,
        out_shape=jax.ShapeDtypeStruct(part.shape, BF16),
        in_specs=[VMEM_SPEC],
        out_specs=VMEM_SPEC,
        scratch_shapes=[
            block, block, block, small, small, small, block,
            pltpu.SemaphoreType.DMA((6,)),
            pltpu.SemaphoreType.DMA((6,)),
        ],
        compiler_params=pltpu.CompilerParams(collective_id=2, has_side_effects=True),
        name="reduce",
    )(part)


def on_device(points, grad_out, dest_dev, dest_row, w_qkv, w_out):
    n_dev = lax.axis_size("curve")
    rows, width = points.shape[1:]
    half = PATCH // 2
    to_previous = [(i, (i - 1) % n_dev) for i in range(n_dev)]
    to_next = [(i, (i + 1) % n_dev) for i in range(n_dev)]
    send, meta, slot = pack(dest_dev, dest_row, points[0], grad_out[0], n_dev)
    got, got_meta = exchange((send, meta.reshape(n_dev, 1, 128)), 0, "dispatch")
    got_meta = got_meta.reshape(n_dev, 128)
    low, high = place(got, got_meta, half)
    following = lax.ppermute(low, "curve", to_previous)
    part, igrad_own, igrad_next = patch_backward(high, following, w_qkv, w_out)
    igrad_low = lax.ppermute(igrad_next, "curve", to_next)
    back = pick(igrad_low, igrad_own, got_meta)
    (returned,) = exchange((back,), 1, "giveback")
    result = collect(returned, slot)
    summed = reduce_parts(part.reshape(2, 16, 128, 256)).reshape(4 * width // 256, width, 256)
    weights = jnp.transpose(summed, (1, 0, 2)).reshape(width, 4 * width).astype(F32)
    return (result[None], weights[:, : 3 * width], weights[:, 3 * width :])


def solution(mesh):
    placed = (
        P("dp", "curve", None),
        P("dp", "curve", None),
        P("dp", "curve"),
        P("dp", "curve"),
        P(),
        P(),
    )
    return jax.shard_map(
        on_device,
        mesh=mesh,
        in_specs=placed,
        out_specs=(P("dp", "curve", None), P(), P()),
        check_vma=False,
    )
```

```python
import functools
import math

import jax
import jax.numpy as jnp
from jax import lax
from jax.experimental import pallas as pl
from jax.experimental.pallas import tpu as pltpu
from jax.sharding import PartitionSpec as P

HEADS = 8
PATCH = 512
CAP = 8
MESH = pl.DeviceIdType.MESH
BF16 = jnp.bfloat16
F32 = jnp.float32
I32 = jnp.int32
VMEM_SPEC = pl.BlockSpec(memory_space=pltpu.VMEM)
ANY_SPEC = pl.BlockSpec(memory_space=pl.ANY)


def dot_nn(a, b):
    return lax.dot_general(a, b, (((1,), (0,)), ((), ())), preferred_element_type=F32)


def dot_nt(a, b):
    return lax.dot_general(a, b, (((1,), (1,)), ((), ())), preferred_element_type=F32)


def iota(shape, dim):
    return lax.broadcasted_iota(I32, shape, dim)


def onehot(mask):
    return jnp.where(mask, 1.0, 0.0).astype(BF16)


def signal(barrier, device):
    pl.semaphore_signal(barrier, inc=1, device_id=device, device_id_type=MESH)


def greet_curve(barrier, me, n_dev):
    def greet(k, carry):
        signal(barrier, {"curve": lax.rem(me + k, n_dev)})
        return carry

    lax.fori_loop(1, n_dev, greet, 0)


def remote(src, dst, send_sem, recv_sem, device):
    return pltpu.make_async_remote_copy(
        src_ref=src, dst_ref=dst, send_sem=send_sem, recv_sem=recv_sem,
        device_id=device, device_id_type=MESH,
    )


def wait_bytes(ref, sem):
    pltpu.make_async_copy(ref, ref, sem).wait()


CHUNK = 16


def send_chunk(send, got, send_sem, recv_sem, me, group, n_dev):
    def one(k, carry):
        peer = group * CHUNK + k

        @pl.when(peer != me)
        def _():
            remote(send.at[peer], got.at[me], send_sem, recv_sem, {"curve": peer}).start()

        return carry

    lax.fori_loop(0, CHUNK, one, 0)

def front_kernel(
    dev_ref, row_ref, points_ref, grads_ref, x_ref, g_ref, gotm_ref, slot_ref,
    send_p, send_g, send_m, got_p, got_g, got_m, low_p, low_g, sems,
):
    n_dev, span, width = send_p.shape
    rows = points_ref.shape[0]
    half = rows // 2
    groups = n_dev // CHUNK
    me = lax.axis_index("curve")
    previous = {"curve": lax.rem(me + n_dev - 1, n_dev)}
    barrier = pltpu.get_barrier_semaphore()
    greet_curve(barrier, me, n_dev)

    dev = dev_ref[...]
    mask = iota((n_dev, rows), 0) == dev
    hot = onehot(mask)
    upper = onehot(iota((rows, rows), 0) <= iota((rows, rows), 1))
    running = dot_nn(hot, upper)
    rank = jnp.sum(jnp.where(mask, running, 0.0), axis=0, keepdims=True).astype(I32) - 1
    slot = dev * CAP + rank
    slot_ref[...] = slot

    def make(group):
        ids = iota((CHUNK * CAP, rows), 0) + group * (CHUNK * CAP)
        pick = onehot(ids == slot)
        where = pl.ds(group * CHUNK, CHUNK)
        send_p[where] = dot_nn(pick, points_ref[...]).reshape(CHUNK, CAP, width).astype(BF16)
        send_g[where] = dot_nn(pick, grads_ref[...]).reshape(CHUNK, CAP, width).astype(BF16)

    home = me // CHUNK
    make(home)
    pl.semaphore_wait(barrier, n_dev - 1)

    def step(s, carry):
        make(lax.rem(home + s, groups))
        send_chunk(
            send_p, got_p, sems.at[0, 0], sems.at[1, 0], me, lax.rem(home + s - 1, groups), n_dev
        )
        return carry

    lax.fori_loop(1, groups, step, 0)
    coded = row_ref[...] + 1
    at_rank = iota((128, rows), 0) == rank
    high = jnp.where(at_rank, (coded >> 8).astype(F32), 0.0).astype(BF16)
    low = jnp.where(at_rank, (coded & 255).astype(F32), 0.0).astype(BF16)
    meta = dot_nt(hot, high) * 256.0 + dot_nt(hot, low)
    send_m[...] = meta.reshape(n_dev, 1, 128)
    send_chunk(
        send_p, got_p, sems.at[0, 0], sems.at[1, 0], me, lax.rem(home + groups - 1, groups), n_dev
    )

    def rest(s, carry):
        group = lax.rem(home + s, groups)
        send_chunk(send_m, got_m, sems.at[0, 1], sems.at[1, 1], me, group, n_dev)
        return carry

    def grads(s, carry):
        group = lax.rem(home + s, groups)
        send_chunk(send_g, got_g, sems.at[0, 2], sems.at[1, 2], me, group, n_dev)
        return carry

    lax.fori_loop(0, groups, rest, 0)
    lax.fori_loop(0, groups, grads, 0)
    got_p[me] = send_p[me]
    got_m[me] = send_m[me]
    got_g[me] = send_g[me]

    others = pl.ds(0, n_dev - 1)
    wait_bytes(got_m.at[others], sems.at[1, 1])
    meta = got_m[...].reshape(n_dev, 128)
    gotm_ref[...] = meta
    total = n_dev * span
    coded = jnp.transpose(meta)[:CAP].astype(I32)
    spread = onehot((iota((n_dev, total), 1) >> 3) == iota((n_dev, total), 0))
    high8 = (coded >> 8).astype(F32).astype(BF16)
    low8 = (coded & 255).astype(F32).astype(BF16)
    spreaded = dot_nn(high8, spread) * 256.0 + dot_nn(low8, spread)
    lane = iota((CAP, total), 1)
    row = jnp.sum(
        jnp.where((lane & (CAP - 1)) == iota((CAP, total), 0), spreaded, 0.0), axis=0, keepdims=True
    ).astype(I32) - 1
    place_low = onehot(iota((half, total), 0) == row)
    place_high = onehot(iota((half, total), 0) + half == row)
    parts = ((0, got_p, low_p, x_ref), (2, got_g, low_g, g_ref))
    for index, got_ref, low_ref, out_ref in parts:
        wait_bytes(got_ref.at[others], sems.at[1, index])
        got = got_ref[...].astype(F32).reshape(total, width).astype(BF16)
        low_ref[...] = dot_nn(place_low, got).astype(BF16)
        out_ref[pl.ds(0, half)] = dot_nn(place_high, got).astype(BF16)
        remote(
            low_ref, out_ref.at[pl.ds(half, half)], sems.at[0, 3 + index], sems.at[1, 3 + index],
            previous,
        ).start()
    wait_bytes(send_p.at[others], sems.at[0, 0])
    wait_bytes(send_m.at[others], sems.at[0, 1])
    wait_bytes(send_g.at[others], sems.at[0, 2])
    for index, got_ref, low_ref, out_ref in parts:
        wait_bytes(low_ref, sems.at[0, 3 + index])
        wait_bytes(out_ref.at[pl.ds(half, half)], sems.at[1, 3 + index])


def front(dev, row, points, grads, n_dev):
    rows, width = points.shape
    whole = jax.ShapeDtypeStruct((rows, width), BF16)
    slots = pltpu.VMEM((n_dev, CAP, width), BF16)
    metas = pltpu.VMEM((n_dev, 1, 128), F32)
    lows = pltpu.VMEM((rows // 2, width), BF16)
    return pl.pallas_call(
        front_kernel,
        out_shape=(
            whole,
            whole,
            jax.ShapeDtypeStruct((n_dev, 128), F32),
            jax.ShapeDtypeStruct((1, rows), I32),
        ),
        in_specs=[VMEM_SPEC] * 4,
        out_specs=(VMEM_SPEC,) * 4,
        scratch_shapes=[
            slots, slots, metas, slots, slots, metas, lows, lows,
            pltpu.SemaphoreType.DMA((2, 6)),
        ],
        compiler_params=pltpu.CompilerParams(collective_id=0, has_side_effects=True),
        name="front",
    )(dev, row, points, grads)


def patch_kernel(
    x_s, g_s, wqkv_ref, wout_ref, part_ref, igrad_own_ref, igrad_next_ref,
    q_s, k_s, v_s, ga_s, kt_s, vt_s, gat_s, attnt_s, gqkv_s,
):
    rows, width = x_s.shape
    half = rows // 2
    pairs = width // 128
    scale = 1.0 / math.sqrt(width // HEADS)

    x = x_s[...]
    qkv = dot_nn(x, wqkv_ref[...])
    ga = dot_nt(g_s[...], wout_ref[...])
    for p in range(pairs):
        cols = slice(p * 128, (p + 1) * 128)
        q_s[p] = (qkv[:, cols].astype(BF16).astype(F32) * scale).astype(BF16)
        k = qkv[:, width + p * 128 : width + (p + 1) * 128].astype(BF16)
        v = qkv[:, 2 * width + p * 128 : 2 * width + (p + 1) * 128].astype(BF16)
        g = ga[:, cols].astype(BF16)
        k_s[p] = k
        v_s[p] = v
        ga_s[p] = g
        kt_s[p] = jnp.transpose(k)
        vt_s[p] = jnp.transpose(v)
        gat_s[p] = jnp.transpose(g)

    def body(p, carry):
        q = q_s[p]
        k = k_s[p]
        v = v_s[p]
        g = ga_s[p]
        grad_k = jnp.zeros((rows, 128), F32)
        grad_v = jnp.zeros((rows, 128), F32)
        lane = iota((rows, 128), 1) // 64
        grad_qt = []
        for h in range(2):
            part = slice(h * 64, (h + 1) * 64)
            keep = lane == h
            qh = jnp.where(keep, q.astype(F32), 0.0).astype(BF16)
            gh = jnp.where(keep, g.astype(F32), 0.0).astype(BF16)
            st = dot_nt(k, qh)
            top = jnp.max(st, axis=0, keepdims=True)
            e = jnp.exp(st - top)
            total = jnp.sum(e, axis=0, keepdims=True)
            pt = e * (1.0 / total)
            low = pt.astype(BF16)
            attnt = dot_nn(vt_s[p, part, :], low).astype(BF16)
            attnt_s[p, part, :] = attnt
            delta = jnp.sum(
                attnt.astype(F32) * gat_s[p, part, :].astype(F32), axis=0, keepdims=True
            )
            grad_v += dot_nn(low, gh)
            gpt = dot_nt(v, gh)
            gst = (pt * (gpt - delta)).astype(BF16)
            grad_k += dot_nn(gst, qh)
            grad_qt.append(dot_nn(kt_s[p, part, :], gst))
        gq = jnp.transpose(jnp.concatenate(grad_qt, axis=0) * scale)
        gqkv_s[p] = gq.astype(BF16)
        gqkv_s[pairs + p] = grad_k.astype(BF16)
        gqkv_s[2 * pairs + p] = grad_v.astype(BF16)
        return carry

    lax.fori_loop(0, pairs, body, 0)
    xt = jnp.transpose(x_s[...])
    igrad = jnp.zeros((rows, width), F32)
    for block in range(3 * pairs // 2):
        gq = jnp.concatenate([gqkv_s[2 * block], gqkv_s[2 * block + 1]], axis=1)
        part = dot_nn(xt, gq).astype(BF16)
        part_ref[2 * block] = part[:, :128]
        part_ref[2 * block + 1] = part[:, 128:]
        igrad += dot_nt(gq, wqkv_ref[:, block * 256 : (block + 1) * 256])
    igrad = igrad.astype(BF16)
    igrad_own_ref[...] = igrad[:half]
    igrad_next_ref[...] = igrad[half:]
    attnt = attnt_s[...].reshape(width, rows)
    pout = dot_nn(attnt, g_s[...])
    for block in range(pairs):
        part_ref[3 * pairs + block] = pout[:, block * 128 : (block + 1) * 128].astype(BF16)


def patch_backward(x, g, w_qkv, w_out):
    rows, width = x.shape
    half = rows // 2
    pairs = width // 128
    tall = pltpu.VMEM((pairs, rows, 128), BF16)
    wide = pltpu.VMEM((pairs, 128, rows), BF16)
    return pl.pallas_call(
        patch_kernel,
        out_shape=(
            jax.ShapeDtypeStruct((4 * width // 128, width, 128), BF16),
            jax.ShapeDtypeStruct((half, width), BF16),
            jax.ShapeDtypeStruct((half, width), BF16),
        ),
        in_specs=[VMEM_SPEC] * 4,
        out_specs=(VMEM_SPEC,) * 3,
        scratch_shapes=[
            tall, tall, tall, tall, wide, wide, wide, wide,
            pltpu.VMEM((3 * pairs, rows, 128), BF16),
        ],
        name="patch",
    )(x, g, w_qkv, w_out)


def back_kernel(
    own_ref, next_ref, meta_ref, part_ref, got_ref, out_ref,
    low_s, send_s, r0, b0, r1, b1, r2, b2, r3, a3, a4, a5, back_sem, low_sem, send_sem, recv_sem,
):
    n_dev, span, width = send_s.shape
    half = own_ref.shape[0]
    groups = n_dev // CHUNK
    c = lax.axis_index("curve")
    d = lax.axis_index("dp")
    core = lax.rem(c, 2)
    x = lax.rem(c // 2, 4)
    z = lax.rem(c // 8, 8)
    y = d * 2 + c // 64
    barrier = pltpu.get_barrier_semaphore()

    def at(y_id, z_id, x_id, core_id):
        return {"curve": ((lax.rem(y_id, 2) * 8 + z_id) * 4 + x_id) * 2 + core_id, "dp": y_id // 2}

    def x_at(k):
        return lax.rem(x + k, 4)

    def y_at(k):
        return lax.rem(y + k, 4)

    def z_at(k):
        return lax.rem(z + k, 8)

    greet_curve(barrier, c, n_dev)
    for y_hat in range(2):
        signal(barrier, {"curve": lax.rem(c, 64) + 64 * y_hat, "dp": 1 - d})
    pl.semaphore_wait(barrier, n_dev + 1)

    def go(src, dst, stage, device):
        remote(src, dst, send_sem.at[stage], recv_sem.at[stage], device).start()

    def done(ref, stage):
        wait_bytes(ref, send_sem.at[stage])
        wait_bytes(ref, recv_sem.at[stage])

    def to_x(src, dst, stage):
        for k in range(1, 4):
            go(src(x_at(k)), dst, stage, at(y, z, x_at(k), core))

    def to_y(src, dst, stage):
        for k in range(1, 4):
            go(src(y_at(k)), dst, stage, at(y_at(k), z, x, core))

    partner = at(y, z, x, 1 - core)
    following = {"curve": lax.rem(c + 1, n_dev)}
    hand = remote(next_ref, low_s, low_sem.at[0], low_sem.at[1], following)
    hand.start()
    go(part_ref.at[1 - core], r0, 0, partner)
    hand.wait()

    def give(s):
        group = lax.rem(c // CHUNK + s, groups)
        coded = meta_ref[...].astype(I32)
        total = CHUNK * span
        spread = onehot(
            (iota((total, n_dev), 0) >> 3) + group * CHUNK == iota((total, n_dev), 1)
        )
        high = (coded >> 8).astype(F32).astype(BF16)
        low = (coded & 255).astype(F32).astype(BF16)
        spreaded = dot_nn(spread, high) * 256.0 + dot_nn(spread, low)
        mine = iota((total, 128), 1) == (iota((total, 128), 0) & (CAP - 1))
        row = jnp.sum(jnp.where(mine, spreaded, 0.0), axis=1, keepdims=True).astype(I32) - 1
        lane = iota((total, half), 1)
        block = dot_nn(onehot(lane == row), low_s[...]) + dot_nn(
            onehot(lane + half == row), own_ref[...]
        )
        send_s[pl.ds(group * CHUNK, CHUNK)] = block.reshape(CHUNK, span, width).astype(BF16)

    def give_many(first, last):
        def one(s, carry):
            give(s)
            group = lax.rem(c // CHUNK + s, groups)
            send_chunk(send_s, got_ref, back_sem.at[0], back_sem.at[1], c, group, n_dev)
            return carry

        lax.fori_loop(first, last, one, 0)

    give_many(0, 1)
    done(r0, 0)

    def add_first(i, carry):
        for h in range(2):
            for j in range(4):
                total = part_ref[core, h, i, j].astype(F32) + r0[h, i, j].astype(F32)
                b0[h, i, j] = total.astype(BF16)
        return carry

    lax.fori_loop(0, 4, add_first, 0)
    r1[0, x] = b0[0, x]
    r1[1, y] = b0[1, y]
    to_x(lambda p: b0.at[0, p], r1.at[0, x], 1)
    to_y(lambda p: b0.at[1, p], r1.at[1, y], 2)
    give_many(1, 3)
    done(r1.at[0, pl.ds(0, 3)], 1)
    done(r1.at[1, pl.ds(0, 3)], 2)
    for h in range(2):
        for j in range(4):
            total = r1[h, 0, j].astype(F32)
            for i in range(1, 4):
                total += r1[h, i, j].astype(F32)
            b1[h, j] = total.astype(BF16)
    r2[0, y] = b1[0, y]
    r2[1, x] = b1[1, x]
    to_y(lambda p: b1.at[0, p], r2.at[0, y], 3)
    to_x(lambda p: b1.at[1, p], r2.at[1, x], 4)
    give_many(3, 5)
    done(r2.at[0, pl.ds(0, 3)], 3)
    done(r2.at[1, pl.ds(0, 3)], 4)
    for h in range(2):
        total = r2[h, 0].astype(F32)
        for i in range(1, 4):
            total += r2[h, i].astype(F32)
        b2[:, h] = total.reshape(8, 16, 128).astype(BF16)
    r3[z] = b2[z]
    for k in range(1, 8):
        go(b2.at[z_at(k)], r3.at[z], 5, at(y, z_at(k), x, core))
    give_many(5, groups)
    done(r3.at[pl.ds(0, 7)], 5)
    final = r3[0].astype(F32)
    for k in range(1, 8):
        final += r3[k].astype(F32)
    a3[z] = final.astype(BF16)
    for k in range(1, 8):
        go(a3.at[z], a3.at[z], 6, at(y, z_at(k), x, core))
    got_ref[c] = send_s[c]
    done(a3.at[pl.ds(0, 7)], 6)
    a4[0, y] = a3[:, 0].reshape(128, 128)
    a4[1, x] = a3[:, 1].reshape(128, 128)
    to_y(lambda p: a4.at[0, y], a4.at[0, y], 7)
    to_x(lambda p: a4.at[1, x], a4.at[1, x], 8)
    done(a4.at[0, pl.ds(0, 3)], 7)
    done(a4.at[1, pl.ds(0, 3)], 8)
    a5[0, x] = a4[0]
    a5[1, y] = a4[1]
    to_x(lambda p: a5.at[0, x], a5.at[0, x], 9)
    to_y(lambda p: a5.at[1, y], a5.at[1, y], 10)
    done(a5.at[0, pl.ds(0, 3)], 9)
    done(a5.at[1, pl.ds(0, 3)], 10)
    go(a5, out_ref.at[core], 11, partner)
    out_ref[core] = a5[...]
    others = pl.ds(0, n_dev - 1)
    wait_bytes(send_s.at[others], back_sem.at[0])
    wait_bytes(got_ref.at[others], back_sem.at[1])
    done(a5, 11)


def back(igrad_own, igrad_next, meta, part):
    n_dev = meta.shape[0]
    half, width = igrad_own.shape
    slots = (n_dev, CAP, width)
    big = pltpu.VMEM((2, 4, 4, 128, 128), BF16)
    mid = pltpu.VMEM((2, 4, 128, 128), BF16)
    small = pltpu.VMEM((8, 2, 16, 128), BF16)
    return pl.pallas_call(
        back_kernel,
        out_shape=(
            jax.ShapeDtypeStruct(slots, BF16),
            jax.ShapeDtypeStruct(part.shape, BF16),
        ),
        in_specs=[VMEM_SPEC] * 4,
        out_specs=(VMEM_SPEC,) * 2,
        scratch_shapes=[
            pltpu.VMEM((half, width), BF16),
            pltpu.VMEM(slots, BF16),
            big, big, big, mid, mid, small, small, small, mid, big,
            pltpu.SemaphoreType.DMA((2,)),
            pltpu.SemaphoreType.DMA((2,)),
            pltpu.SemaphoreType.DMA((12,)),
            pltpu.SemaphoreType.DMA((12,)),
        ],
        compiler_params=pltpu.CompilerParams(collective_id=1, has_side_effects=True),
        name="back",
    )(igrad_own, igrad_next, meta, part)


def finish_kernel(got_ref, slot_ref, sum_ref, out_ref, wqkv_ref, wout_ref):
    n_dev, span, width = got_ref.shape
    rows = out_ref.shape[0]
    total = n_dev * span
    slot = jnp.transpose(jnp.broadcast_to(slot_ref[...].astype(F32), (128, rows)))[:, :1]
    hot = onehot(iota((rows, total), 1) == slot.astype(I32))
    got = got_ref[...].astype(F32).reshape(total, width).astype(BF16)
    out_ref[...] = dot_nn(hot, got).astype(BF16)
    blocks = 3 * width // 128
    for block in range(blocks):
        wqkv_ref[:, block * 128 : (block + 1) * 128] = sum_ref[block].astype(F32)
    for block in range(width // 128):
        wout_ref[:, block * 128 : (block + 1) * 128] = sum_ref[blocks + block].astype(F32)


def finish(got, slot, summed):
    rows = slot.shape[1]
    width = got.shape[2]
    return pl.pallas_call(
        finish_kernel,
        out_shape=(
            jax.ShapeDtypeStruct((rows, width), BF16),
            jax.ShapeDtypeStruct((width, 3 * width), F32),
            jax.ShapeDtypeStruct((width, width), F32),
        ),
        in_specs=[VMEM_SPEC] * 3,
        out_specs=(VMEM_SPEC,) * 3,
        name="finish",
    )(got, slot, summed)


def on_device(points, grad_out, dest_dev, dest_row, w_qkv, w_out):
    n_dev = lax.axis_size("curve")
    width = points.shape[2]
    x, g, meta, slot = front(dest_dev, dest_row, points[0], grad_out[0], n_dev)
    part, igrad_own, igrad_next = patch_backward(x, g, w_qkv, w_out)
    got, summed = back(igrad_own, igrad_next, meta, part.reshape(2, 2, 4, 4, 128, 128))
    result, weight_qkv, weight_out = finish(got, slot, summed.reshape(4 * width // 128, width, 128))
    return (result[None], weight_qkv, weight_out)


def solution(mesh):
    placed = (
        P("dp", "curve", None),
        P("dp", "curve", None),
        P("dp", "curve"),
        P("dp", "curve"),
        P(),
        P(),
    )
    return jax.shard_map(
        on_device,
        mesh=mesh,
        in_specs=placed,
        out_specs=(P("dp", "curve", None), P(), P()),
        check_vma=False,
    )
```

```python
import functools
import math

import jax
import jax.numpy as jnp
from jax import lax
from jax.experimental import pallas as pl
from jax.experimental.pallas import tpu as pltpu
from jax.sharding import PartitionSpec as P

HEADS = 8
PATCH = 512
CAP = 8
MESH = pl.DeviceIdType.MESH
BF16 = jnp.bfloat16
F32 = jnp.float32
I32 = jnp.int32
VMEM_SPEC = pl.BlockSpec(memory_space=pltpu.VMEM)
ANY_SPEC = pl.BlockSpec(memory_space=pl.ANY)


def dot_nn(a, b):
    return lax.dot_general(a, b, (((1,), (0,)), ((), ())), preferred_element_type=F32)


def dot_nt(a, b):
    return lax.dot_general(a, b, (((1,), (1,)), ((), ())), preferred_element_type=F32)


def iota(shape, dim):
    return lax.broadcasted_iota(I32, shape, dim)


def onehot(mask):
    return jnp.where(mask, 1.0, 0.0).astype(BF16)


def signal(barrier, device):
    pl.semaphore_signal(barrier, inc=1, device_id=device, device_id_type=MESH)


def greet_curve(barrier, me, n_dev):
    def greet(k, carry):
        signal(barrier, {"curve": lax.rem(me + k, n_dev)})
        return carry

    lax.fori_loop(1, n_dev, greet, 0)


def remote(src, dst, send_sem, recv_sem, device):
    return pltpu.make_async_remote_copy(
        src_ref=src, dst_ref=dst, send_sem=send_sem, recv_sem=recv_sem,
        device_id=device, device_id_type=MESH,
    )


def wait_bytes(ref, sem):
    pltpu.make_async_copy(ref, ref, sem).wait()


CHUNK = 16


def send_chunk(send, got, send_sem, recv_sem, me, group, n_dev):
    def one(k, carry):
        peer = group * CHUNK + k

        @pl.when(peer != me)
        def _():
            remote(send.at[peer], got.at[me], send_sem, recv_sem, {"curve": peer}).start()

        return carry

    lax.fori_loop(0, CHUNK, one, 0)


def spread_rows(meta, span):
    n_dev = meta.shape[0]
    total = n_dev * span
    coded = jnp.transpose(meta)[:CAP].astype(I32)
    spread = onehot((iota((n_dev, total), 1) >> 3) == iota((n_dev, total), 0))
    high = (coded >> 8).astype(F32).astype(BF16)
    low = (coded & 255).astype(F32).astype(BF16)
    values = dot_nn(high, spread) * 256.0 + dot_nn(low, spread)
    mine = (iota((CAP, total), 1) & (CAP - 1)) == iota((CAP, total), 0)
    return jnp.sum(jnp.where(mine, values, 0.0), axis=0, keepdims=True).astype(I32) - 1


def layer_kernel(
    dev_ref, row_ref, points_ref, grads_ref, wqkv_ref, wout_ref,
    slot_ref, back_ref, out_ref,
    send_p, send_g, send_m, got_p, got_g, got_m, send_s, place_lo, place_hi, pick_lo, pick_hi,
    x_s, g_s, low_p, low_g, hand_s, low_s, own_s,
    q_s, k_s, v_s, ga_s, kt_s, vt_s, gat_s, attnt_s, xt_s, pt_s, ig_s,
    part_s, r0, b0, r1, b1, r2, a3, a5,
    snd, rcv,
):
    n_dev, span, width = send_p.shape
    rows = points_ref.shape[0]
    half = rows // 2
    total = n_dev * span
    groups = n_dev // CHUNK
    pairs = width // 128
    scale = 1.0 / math.sqrt(width // HEADS)
    others = pl.ds(0, n_dev - 1)
    c = lax.axis_index("curve")
    d = lax.axis_index("dp")
    core = lax.rem(c, 2)
    x = lax.rem(c // 2, 4)
    z = lax.rem(c // 8, 8)
    y = d * 2 + c // 64

    def at(y_id, z_id, x_id, core_id):
        return {"curve": ((lax.rem(y_id, 2) * 8 + z_id) * 4 + x_id) * 2 + core_id, "dp": y_id // 2}

    partner = at(y, z, x, 1 - core)
    previous = {"curve": lax.rem(c + n_dev - 1, n_dev)}
    following = {"curve": lax.rem(c + 1, n_dev)}

    barrier = pltpu.get_barrier_semaphore()
    greet_curve(barrier, c, n_dev)

    def greet_other(k, carry):
        curve = ((k // 8) * 8 + lax.rem(k, 8)) * 8 + x * 2 + core
        signal(barrier, {"curve": curve, "dp": 1 - d})
        return carry

    lax.fori_loop(0, 16, greet_other, 0)

    dev = dev_ref[...]
    mask = iota((n_dev, rows), 0) == dev
    hot = onehot(mask)
    upper = onehot(iota((rows, rows), 0) <= iota((rows, rows), 1))
    running = dot_nn(hot, upper)
    rank = jnp.sum(jnp.where(mask, running, 0.0), axis=0, keepdims=True).astype(I32) - 1
    slot = dev * CAP + rank
    slot_ref[...] = slot
    coded = row_ref[...] + 1
    at_rank = iota((128, rows), 0) == rank
    high = jnp.where(at_rank, (coded >> 8).astype(F32), 0.0).astype(BF16)
    low = jnp.where(at_rank, (coded & 255).astype(F32), 0.0).astype(BF16)
    meta = dot_nt(hot, high) * 256.0 + dot_nt(hot, low)
    send_m[...] = meta.reshape(n_dev, 1, 128)

    def make(group):
        ids = iota((CHUNK * CAP, rows), 0) + group * (CHUNK * CAP)
        pick = onehot(ids == slot)
        where = pl.ds(group * CHUNK, CHUNK)
        send_p[where] = dot_nn(pick, points_ref[...]).reshape(CHUNK, CAP, width).astype(BF16)
        send_g[where] = dot_nn(pick, grads_ref[...]).reshape(CHUNK, CAP, width).astype(BF16)

    home = c // CHUNK
    make(home)
    pl.semaphore_wait(barrier, n_dev + 15)

    def send_meta(s, carry):
        send_chunk(send_m, got_m, snd.at[0], rcv.at[0], c, lax.rem(home + s, groups), n_dev)
        return carry

    lax.fori_loop(0, groups, send_meta, 0)

    def send_points(s, carry):
        make(lax.rem(home + s, groups))
        send_chunk(send_p, got_p, snd.at[1], rcv.at[1], c, lax.rem(home + s - 1, groups), n_dev)
        return carry

    lax.fori_loop(1, groups, send_points, 0)
    last = lax.rem(home + groups - 1, groups)
    send_chunk(send_p, got_p, snd.at[1], rcv.at[1], c, last, n_dev)

    def send_grads(s, carry):
        send_chunk(send_g, got_g, snd.at[2], rcv.at[2], c, lax.rem(home + s, groups), n_dev)
        return carry

    lax.fori_loop(0, groups, send_grads, 0)
    got_m[c] = send_m[c]
    got_p[c] = send_p[c]
    got_g[c] = send_g[c]

    wait_bytes(got_m.at[others], rcv.at[0])
    row = spread_rows(got_m[...].reshape(n_dev, 128), span)
    place_lo[...] = onehot(iota((half, total), 0) == row)
    place_hi[...] = onehot(iota((half, total), 0) + half == row)
    pick_lo[...] = jnp.transpose(place_lo[...])
    pick_hi[...] = jnp.transpose(place_hi[...])

    def place(got_ref, low_ref, out_ref, index):
        got = got_ref[...].astype(F32).reshape(total, width).astype(BF16)
        low_ref[...] = dot_nn(place_lo[...], got).astype(BF16)
        shift = remote(
            low_ref, out_ref.at[pl.ds(half, half)], snd.at[index], rcv.at[index], previous
        )
        shift.start()
        out_ref[pl.ds(0, half)] = dot_nn(place_hi[...], got).astype(BF16)
        return shift

    wait_bytes(got_p.at[others], rcv.at[1])
    shift_p = place(got_p, low_p, x_s, 3)

    def project(first):
        part = slice(first, first + half)
        qkv = dot_nn(x_s[part], wqkv_ref[...])
        for p in range(pairs):
            cols = slice(p * 128, (p + 1) * 128)
            q_s[p, part] = (qkv[:, cols].astype(BF16).astype(F32) * scale).astype(BF16)
            k = qkv[:, width + p * 128 : width + (p + 1) * 128].astype(BF16)
            v = qkv[:, 2 * width + p * 128 : 2 * width + (p + 1) * 128].astype(BF16)
            k_s[p, part] = k
            v_s[p, part] = v
            kt_s[p, :, part] = jnp.transpose(k)
            vt_s[p, :, part] = jnp.transpose(v)

    project(0)
    shift_p.wait()
    project(half)
    xt_s[...] = jnp.transpose(x_s[...])

    def keep_head(value, h):
        lane = iota((rows, 128), 1) // 64
        return jnp.where(lane == h, value.astype(F32), 0.0).astype(BF16)

    def forward(p, carry):
        for h in range(2):
            part = slice(h * 64, (h + 1) * 64)
            st = dot_nt(k_s[p], keep_head(q_s[p], h))
            e = jnp.exp(st - jnp.max(st, axis=0, keepdims=True))
            pt = e * (1.0 / jnp.sum(e, axis=0, keepdims=True))
            pt_s[p, h] = pt
            attnt_s[p, part, :] = dot_nn(vt_s[p, part, :], pt.astype(BF16)).astype(BF16)
        return carry

    lax.fori_loop(0, pairs, forward, 0)

    wait_bytes(got_g.at[others], rcv.at[2])
    shift_g = place(got_g, low_g, g_s, 4)

    def project_grads(first):
        part = slice(first, first + half)
        ga = dot_nt(g_s[part], wout_ref[...])
        for p in range(pairs):
            g = ga[:, p * 128 : (p + 1) * 128].astype(BF16)
            ga_s[p, part] = g
            gat_s[p, :, part] = jnp.transpose(g)

    project_grads(0)
    ig_s[...] = jnp.zeros((rows, width), F32)
    shift_g.wait()
    project_grads(half)

    def core_copy(first, count, index):
        where = pl.ds(first, count)
        return remote(
            part_s.at[1 - core, where], r0.at[where], snd.at[8 + index], rcv.at[8 + index], partner
        )

    def add_blocks(first, count, index):
        core_copy(first, count, index).wait()
        for j in range(count):
            value = part_s[core, first + j].astype(F32) + r0[first + j].astype(F32)
            b0[first + j] = value.astype(BF16)

    def line_at(h, k):
        return lax.rem((y if h else x) + k, 4)

    def line_peer(h, k):
        return at(line_at(1, k), z, x, core) if h else at(y, z, line_at(0, k), core)

    def start_first(h):
        mine = y if h else x
        r1[h, mine] = b0[pl.ds(8 * h + 2 * mine, 2)]
        for k in range(1, 4):
            source = b0.at[pl.ds(8 * h + 2 * line_at(h, k), 2)]
            remote(source, r1.at[h, mine], snd.at[16 + h], rcv.at[16 + h], line_peer(h, k)).start()

    pout = dot_nn(attnt_s[...].reshape(width, rows), g_s[...]).astype(BF16)
    for j in range(pairs):
        cols = slice(j * 128, (j + 1) * 128)
        part_s[0, j] = pout[:half, cols]
        part_s[1, j] = pout[half:, cols]
    core_copy(0, pairs, pairs).start()

    def backward(p, carry):
        k = k_s[p]
        v = v_s[p]
        grad_k = jnp.zeros((rows, 128), F32)
        grad_v = jnp.zeros((rows, 128), F32)
        grad_qt = []
        for h in range(2):
            part = slice(h * 64, (h + 1) * 64)
            qh = keep_head(q_s[p], h)
            gh = keep_head(ga_s[p], h)
            delta = jnp.sum(
                attnt_s[p, part, :].astype(F32) * gat_s[p, part, :].astype(F32),
                axis=0, keepdims=True,
            )
            pt = pt_s[p, h]
            grad_v += dot_nn(pt.astype(BF16), gh)
            gst = (pt * (dot_nt(v, gh) - delta)).astype(BF16)
            grad_k += dot_nn(gst, qh)
            grad_qt.append(dot_nn(kt_s[p, part, :], gst))
        grad_q = jnp.transpose(jnp.concatenate(grad_qt, axis=0) * scale)
        blocks = [grad_q.astype(BF16), grad_k.astype(BF16), grad_v.astype(BF16)]
        joined = jnp.concatenate(blocks, axis=1)
        part = dot_nn(xt_s[...], joined).astype(BF16)
        for j in range(3):
            cols = slice(j * 128, (j + 1) * 128)
            part_s[0, pairs + 3 * p + j] = part[:half, cols]
            part_s[1, pairs + 3 * p + j] = part[half:, cols]
        core_copy(pairs + 3 * p, 3, p).start()
        weights = [
            wqkv_ref[:, pl.ds(pl.multiple_of(j * width + p * 128, 128), 128)] for j in range(3)
        ]
        ig_s[...] += dot_nt(joined, jnp.concatenate(weights, axis=1))

        @pl.when(p == 0)
        def _():
            add_blocks(0, pairs, pairs)

        @pl.when(p > 0)
        def _():
            add_blocks(pairs + 3 * (p - 1), 3, p - 1)

        @pl.when(p == 2)
        def _():
            start_first(0)

        return carry

    lax.fori_loop(0, pairs, backward, 0)

    hand_s[...] = ig_s[pl.ds(half, half)].astype(BF16)
    hand = remote(hand_s, low_s, snd.at[5], rcv.at[5], following)
    hand.start()
    own_s[...] = ig_s[pl.ds(0, half)].astype(BF16)
    add_blocks(pairs + 3 * (pairs - 1), 3, pairs - 1)
    start_first(1)
    hand.wait()

    def give_many(first, last):
        def one(s, carry):
            group = lax.rem(home + s, groups)
            some = pl.ds(pl.multiple_of(group * CHUNK * CAP, CHUNK * CAP), CHUNK * CAP)
            block = dot_nn(pick_lo[some], low_s[...]) + dot_nn(pick_hi[some], own_s[...])
            send_s[pl.ds(group * CHUNK, CHUNK)] = block.reshape(CHUNK, span, width).astype(BF16)
            send_chunk(send_s, back_ref, snd.at[6], rcv.at[6], c, group, n_dev)
            return carry

        lax.fori_loop(first, last, one, 0)

    def three(ref, index):
        wait_bytes(ref.at[pl.ds(0, 3)], snd.at[index])
        wait_bytes(ref.at[pl.ds(0, 3)], rcv.at[index])

    def sheet_mine(h):
        return (x if h else y) * 8 + z

    def sheet_loop(h, source, target, index):
        def one(k, carry):
            peer = lax.rem(sheet_mine(h) + k, 32)
            line = peer // 8
            device = at(y, lax.rem(peer, 8), line, core) if h else at(line, lax.rem(peer, 8), x, core)
            remote(source(peer), target, snd.at[index], rcv.at[index], device).start()
            return carry

        lax.fori_loop(1, 32, one, 0)

    def sheet_wait(ref, index):
        wait_bytes(ref.at[pl.ds(0, 31)], snd.at[index])
        wait_bytes(ref.at[pl.ds(0, 31)], rcv.at[index])

    def second(h):
        three(r1.at[h], 16 + h)
        value = r1[h, 0].astype(F32)
        for i in range(1, 4):
            value += r1[h, i].astype(F32)
        b1[h] = value.astype(BF16).reshape(32, 16, 128)
        mine = sheet_mine(h)
        r2[h, mine] = b1[h, mine]
        sheet_loop(h, lambda peer: b1.at[h, peer], r2.at[h, mine], 18 + h)

    def third(h):
        sheet_wait(r2.at[h], 18 + h)
        mine = sheet_mine(h)
        a3[h, mine] = jnp.sum(r2[h].astype(F32), axis=0).astype(BF16)
        sheet_loop(h, lambda peer: a3.at[h, mine], a3.at[h, mine], 20 + h)

    def forward_piece(h, i):
        remote(a5.at[h, i], out_ref.at[core, h, i], snd.at[7], rcv.at[7], partner).start()

    def fourth(h):
        sheet_wait(a3.at[h], 20 + h)
        mine = y if h else x
        a5[h, mine] = a3[h]
        for k in range(1, 4):
            remote(
                a5.at[h, mine], a5.at[h, mine], snd.at[22 + h], rcv.at[24 + 4 * h + k],
                line_peer(h, k),
            ).start()
        forward_piece(h, mine)

    give_many(0, 2)
    second(0)
    give_many(2, 4)
    second(1)
    third(0)
    give_many(4, 6)
    third(1)
    give_many(6, groups)
    back_ref[c] = send_s[c]
    fourth(0)
    fourth(1)
    for k in range(1, 4):
        for h in range(2):
            piece = lax.rem((y if h else x) + 4 - k, 4)
            wait_bytes(a5.at[h, piece], rcv.at[24 + 4 * h + k])
            forward_piece(h, piece)
    out_ref[core] = a5[...]
    for h in range(2):
        wait_bytes(a5.at[h, pl.ds(0, 3)], snd.at[22 + h])
    wait_bytes(send_m.at[others], snd.at[0])
    wait_bytes(send_p.at[others], snd.at[1])
    wait_bytes(send_g.at[others], snd.at[2])
    wait_bytes(send_s.at[others], snd.at[6])
    wait_bytes(back_ref.at[others], rcv.at[6])
    wait_bytes(a5, snd.at[7])
    wait_bytes(a5, rcv.at[7])


def layer(dev, row, points, grads, w_qkv, w_out, n_dev):
    rows, width = points.shape
    half = rows // 2
    total = n_dev * CAP
    pairs = width // 128
    slots = pltpu.VMEM((n_dev, CAP, width), BF16)
    metas = pltpu.VMEM((n_dev, 1, 128), F32)
    whole = pltpu.VMEM((rows, width), BF16)
    halves = pltpu.VMEM((half, width), BF16)
    tall = pltpu.VMEM((pairs, rows, 128), BF16)
    wide = pltpu.VMEM((pairs, 128, rows), BF16)
    blocks = pltpu.VMEM((16, 256, 128), BF16)
    sheets = pltpu.VMEM((2, 32, 16, 128), BF16)
    return pl.pallas_call(
        layer_kernel,
        out_shape=(
            jax.ShapeDtypeStruct((1, rows), I32),
            jax.ShapeDtypeStruct((n_dev, CAP, width), BF16),
            jax.ShapeDtypeStruct((2, 2, 4, 32, 16, 128), BF16),
        ),
        in_specs=[VMEM_SPEC] * 6,
        out_specs=(VMEM_SPEC,) * 3,
        scratch_shapes=[
            slots, slots, metas, slots, slots, metas, slots,
            pltpu.VMEM((half, total), BF16),
            pltpu.VMEM((half, total), BF16),
            pltpu.VMEM((total, half), BF16),
            pltpu.VMEM((total, half), BF16),
            whole, whole, halves, halves, halves, halves, halves,
            tall, tall, tall, tall, wide, wide, wide, wide, whole,
            pltpu.VMEM((pairs, 2, rows, rows), F32),
            pltpu.VMEM((rows, width), F32),
            pltpu.VMEM((2, 16, 256, 128), BF16),
            blocks, blocks,
            pltpu.VMEM((2, 4, 2, 256, 128), BF16),
            sheets, sheets, sheets,
            pltpu.VMEM((2, 4, 32, 16, 128), BF16),
            pltpu.SemaphoreType.DMA((24,)),
            pltpu.SemaphoreType.DMA((32,)),
        ],
        compiler_params=pltpu.CompilerParams(collective_id=0, has_side_effects=True),
        name="layer",
    )(dev, row, points, grads, w_qkv, w_out)


def finish_kernel(got_ref, slot_ref, sum_ref, out_ref, wqkv_ref, wout_ref):
    n_dev, span, width = got_ref.shape
    rows = out_ref.shape[0]
    total = n_dev * span
    slot = jnp.transpose(jnp.broadcast_to(slot_ref[...].astype(F32), (128, rows)))[:, :1]
    hot = onehot(iota((rows, total), 1) == slot.astype(I32))
    got = got_ref[...].astype(F32).reshape(total, width).astype(BF16)
    out_ref[...] = dot_nn(hot, got).astype(BF16)
    pairs = width // 128
    for j in range(pairs):
        wout_ref[:, j * 128 : (j + 1) * 128] = sum_ref[0, j].astype(F32)
    for p in range(pairs):
        for j in range(3):
            first = j * width + p * 128
            wqkv_ref[:, first : first + 128] = sum_ref[0, pairs + 3 * p + j].astype(F32)


def finish(got, slot, summed):
    rows = slot.shape[1]
    width = got.shape[2]
    step = 128
    return pl.pallas_call(
        finish_kernel,
        out_shape=(
            jax.ShapeDtypeStruct((rows, width), BF16),
            jax.ShapeDtypeStruct((width, 3 * width), F32),
            jax.ShapeDtypeStruct((width, width), F32),
        ),
        grid=(rows // step,),
        in_specs=[
            pl.BlockSpec(got.shape, lambda i: (0, 0, 0)),
            pl.BlockSpec((1, step), lambda i: (0, i)),
            pl.BlockSpec((1, 16, step, 128), lambda i: (i // 2, 0, i % 2, 0)),
        ],
        out_specs=(
            pl.BlockSpec((step, width), lambda i: (i, 0)),
            pl.BlockSpec((step, 3 * width), lambda i: (i, 0)),
            pl.BlockSpec((step, width), lambda i: (i, 0)),
        ),
        name="finish",
    )(got, slot, summed)


def on_device(points, grad_out, dest_dev, dest_row, w_qkv, w_out):
    n_dev = lax.axis_size("curve")
    slot, got, summed = layer(
        dest_dev, dest_row, points[0], grad_out[0], w_qkv, w_out, n_dev
    )
    result, weight_qkv, weight_out = finish(got, slot, summed.reshape(2, 16, 256, 128))
    return (result[None], weight_qkv, weight_out)


def solution(mesh):
    placed = (
        P("dp", "curve", None),
        P("dp", "curve", None),
        P("dp", "curve"),
        P("dp", "curve"),
        P(),
        P(),
    )
    return jax.shard_map(
        on_device,
        mesh=mesh,
        in_specs=placed,
        out_specs=(P("dp", "curve", None), P(), P()),
        check_vma=False,
    )
```
